512 devices in a mesh: seq: 64 (over z, y), req: 8 (over x, core).
Axes of the slice: x: 4, y: 8, z: 8, core: 2. Of those that a mesh axis runs over, the one named last changes fastest.
Arguments:
- hidden_in: bfloat16 [128, 4, 2048], P('req'), may hold values from -6 to 6
- attn_gain: float32 [2048], replicated, may hold values from 0.5 to 1.5
- q_gain: float32 [256], replicated, may hold values from 0.5 to 1.5
- k_gain: float32 [256], replicated, may hold values from 0.5 to 1.5
- post_attn_gain: float32 [2048], replicated, may hold values from 0.5 to 1.5
- ffn_gain: float32 [2048], replicated, may hold values from 0.5 to 1.5
- post_ffn_gain: float32 [2048], replicated, may hold values from 0.5 to 1.5
- w_qkv: bfloat16 [2048, 3072], P('seq', 'req'), may hold values from -0.125 to 0.125
- w_out: bfloat16 [2048, 2048], P('seq', 'req'), may hold values from -0.125 to 0.125
- w_gate: bfloat16 [2048, 8192], P('req', 'seq'), may hold values from -0.125 to 0.125
- w_up: bfloat16 [2048, 8192], P('req', 'seq'), may hold values from -0.125 to 0.125
- w_down: bfloat16 [8192, 2048], P('seq', 'req'), may hold values from -0.0625 to 0.0625
- prompt_keys: bfloat16 [16, 8192, 512], P('req', 'seq')
- prompt_values: bfloat16 [16, 8192, 512], P('req', 'seq'), may hold values from -6 to 6
- tail_keys: bfloat16 [8, 16384, 512], P('req', 'seq')
- tail_values: bfloat16 [8, 16384, 512], P('req', 'seq'), may hold values from -6 to 6
- group_of: int32 [128], P('req'), may hold values from 0 to 15, as said below
- prompt_lengths: int32 [16], P('req'), may hold values from 1 to 8192
- tail_lengths: int32 [128], P('req'), may hold values from 1 to 1024
- page_table: int32 [8, 1024], P('req'), may hold values from 0 to 1023, each once within a row
Outputs:
- layer_out: bfloat16 [128, 4, 2048], P('req')
The draws below stay inside these ranges and needn't reach their ends.
Inputs may be any that keep to these rules, and one draw needn't show every extreme that they name: `group_of`: request i belongs to one of the 2 groups i // 16 * 2 to i // 16 * 2 + 1 of its own block of requests. `page_table`: each row lists every pool page of its index of req once; entry j * 64 + p is the pool page of page p of the j-th request of that block.
All inputs are finite; a program needn't handle non-finite values.
Results may differ from the reference program's by a relative error of at most 0.012.
The reference program's roundings to bfloat16 on the way count: a program that leaves them out, or rounds other values in their place, can miss the bound.
Values may be sent and summed in bfloat16 or wider, within the bound.
A program may use at most 128 MiB of HBM per device.

```python
import jax
import jax.numpy as jnp
from jax import lax

D = 2048
H = 8
KV = 2
HD = 256
FF = 8192
REQ_DEV = 16
STEPS = 4
GROUPS_DEV = 2
PROMPT_DEV = 128
PAGE = 16
SLOTS = 16
QKV = 3072
REQUESTS = 128
GROUPS = 16
PROMPT_MAX = 8192
POOL = 16384
TAIL_PAGES = 64
N_SEQ = 64
N_REQ = 8


def scaled_keys(key, shape):
    base = jax.random.normal(key, shape, jnp.float32)
    return 0.25 * base


def draw_prompt_keys(key, part):
    return scaled_keys(key, (GROUPS, PROMPT_MAX, KV * HD)).astype(jnp.bfloat16)


def draw_tail_keys(key, part):
    return scaled_keys(key, (N_REQ, POOL, KV * HD)).astype(jnp.bfloat16)


def draw_group_of(key, part):
    picked = jax.random.randint(key, (N_REQ, REQ_DEV), 0, GROUPS_DEV, dtype=jnp.int32)
    other = (picked[:, 0] + 1) % GROUPS_DEV
    picked = picked.at[:, REQ_DEV - 1].set(other)
    block_base = jnp.arange(N_REQ, dtype=jnp.int32)[:, None] * GROUPS_DEV
    return (block_base + picked).reshape(REQUESTS).astype(jnp.int32)


def place_ends(drawn, stream_key, low, largest):
    longest = drawn.shape.index(max(drawn.shape))
    spots = []
    for shift in (0, 1):
        where = [jax.random.randint(jax.random.fold_in(stream_key, axis), (), 0, length) for axis, length in enumerate(drawn.shape)]
        where[longest] = (where[longest] + shift) % drawn.shape[longest]
        spots.append(tuple(where))
    return drawn.at[spots[0]].set(low).at[spots[1]].set(largest)


def block_levels(own_key, shape, shards, least, largest):
    level = 1.0
    for dim, shards_of in shards:
        steps = jax.random.uniform(jax.random.fold_in(jax.random.fold_in(own_key, 6), dim), (shards_of,), jnp.float32, least / len(shards), largest / len(shards))
        level = level * jnp.repeat(jnp.exp(steps), shape[dim] // shards_of).reshape((-1,) + (1,) * (len(shape) - 1 - dim))
    return level


def bell_draw(key, dims, width, reach, shards=(), held_as=jnp.bfloat16):
    result = width * jax.random.normal(key, dims, jnp.float32)
    if shards:
        result = result * block_levels(key, dims, shards, -0.22, 0.18)
    return jnp.clip(result, -reach, reach).astype(held_as)


def setup_inputs(seed: int = 0) -> dict:
    seeds = jax.random.split(jax.random.key(seed), 21)
    return {
        "hidden_in": bell_draw(seeds[0], (REQUESTS, STEPS, D), 1.0, 6.0, ((0, 8),)),
        "attn_gain": jnp.clip(jax.random.uniform(seeds[1], (D,), jnp.float32, 0.5, 1.5), 0.5, 1.5),
        "q_gain": jnp.clip(jax.random.uniform(seeds[2], (HD,), jnp.float32, 0.5, 1.5), 0.5, 1.5),
        "k_gain": jnp.clip(jax.random.uniform(seeds[3], (HD,), jnp.float32, 0.5, 1.5), 0.5, 1.5),
        "post_attn_gain": jnp.clip(jax.random.uniform(seeds[4], (D,), jnp.float32, 0.5, 1.5), 0.5, 1.5),
        "ffn_gain": jnp.clip(jax.random.uniform(seeds[5], (D,), jnp.float32, 0.5, 1.5), 0.5, 1.5),
        "post_ffn_gain": jnp.clip(jax.random.uniform(seeds[6], (D,), jnp.float32, 0.5, 1.5), 0.5, 1.5),
        "w_qkv": bell_draw(seeds[7], (D, QKV), D ** -0.5, 0.125, ((0, 64), (1, 8))),
        "w_out": bell_draw(seeds[8], (H * HD, D), (H * HD) ** -0.5, 0.125, ((0, 64), (1, 8))),
        "w_gate": bell_draw(seeds[9], (D, FF), D ** -0.5, 0.125, ((0, 8), (1, 64))),
        "w_up": bell_draw(seeds[10], (D, FF), D ** -0.5, 0.125, ((0, 8), (1, 64))),
        "w_down": bell_draw(seeds[11], (FF, D), FF ** -0.5, 0.0625, ((0, 64), (1, 8))),
        "prompt_keys": draw_prompt_keys(jax.random.fold_in(seeds[20], 71), 0),
        "prompt_values": bell_draw(seeds[13], (GROUPS, PROMPT_MAX, KV * HD), 1.0, 6.0, ((0, 8), (1, 64))),
        "tail_keys": draw_tail_keys(jax.random.fold_in(seeds[20], 71), 0),
        "tail_values": bell_draw(seeds[15], (N_REQ, POOL, KV * HD), 1.0, 6.0, ((0, 8), (1, 64))),
        "group_of": draw_group_of(jax.random.fold_in(seeds[20], 71), 0),
        "prompt_lengths": place_ends(jax.random.randint(seeds[17], (GROUPS,), 1, PROMPT_MAX + 1), jax.random.fold_in(seeds[17], 1), 1, PROMPT_MAX).astype(jnp.int32),
        "tail_lengths": place_ends(jax.random.randint(seeds[18], (REQUESTS,), 1, TAIL_PAGES * PAGE + 1), jax.random.fold_in(seeds[18], 1), 1, TAIL_PAGES * PAGE).astype(jnp.int32),
        "page_table": jax.vmap(lambda own: jax.random.permutation(own, N_SEQ * SLOTS))(jax.random.split(seeds[19], N_REQ)).reshape((N_REQ, N_SEQ * SLOTS)).astype(jnp.int32),
    }


EPSILON = 1e-06
NEGATIVE = -1e+30

def normalize(values):
    return values * lax.rsqrt(lax.optimization_barrier(jnp.mean(values * values, axis=-1, keepdims=True)) + EPSILON)

def reference(hidden_in, attn_gain, q_gain, k_gain, post_attn_gain, ffn_gain, post_ffn_gain, w_qkv, w_out, w_gate, w_up, w_down, prompt_keys, prompt_values, tail_keys, tail_values, group_of, prompt_lengths, tail_lengths, page_table):
    group_size = H // KV
    hidden = hidden_in.astype(jnp.float32)
    normed = (normalize(hidden) * attn_gain).astype(jnp.bfloat16)
    projected = jnp.dot(normed.reshape(REQUESTS * STEPS, D), w_qkv, preferred_element_type=jnp.float32).reshape(REQUESTS, STEPS, QKV)
    queries = (normalize(projected[..., :H * HD].reshape(REQUESTS, STEPS, H, HD)) * q_gain).astype(jnp.bfloat16)
    keys_new = (normalize(projected[..., H * HD:(H + KV) * HD].reshape(REQUESTS, STEPS, KV, HD)) * k_gain).astype(jnp.bfloat16)
    values_new = normalize(projected[..., (H + KV) * HD:].reshape(REQUESTS, STEPS, KV, HD)).astype(jnp.bfloat16)
    query_groups = queries.reshape(N_REQ, REQ_DEV, STEPS, KV, group_size, HD).astype(jnp.float32)
    local_group = (group_of % GROUPS_DEV).reshape(N_REQ, REQ_DEV)
    member = local_group[:, :, None] == jnp.arange(GROUPS_DEV, dtype=jnp.int32)[None, None, :]
    prompt_len = prompt_lengths.reshape(N_REQ, GROUPS_DEV)
    tail_len = tail_lengths.reshape(N_REQ, REQ_DEV)
    page_count = N_SEQ * SLOTS
    inverse = jnp.zeros((N_REQ, page_count), jnp.int32).at[jnp.arange(N_REQ, dtype=jnp.int32)[:, None], page_table].set(jnp.arange(page_count, dtype=jnp.int32)[None, :])
    owners_rows = jnp.repeat(inverse // TAIL_PAGES, PAGE, axis=1)
    position_rows = jnp.repeat(inverse % TAIL_PAGES, PAGE, axis=1) * PAGE + jnp.tile(jnp.arange(PAGE, dtype=jnp.int32), page_count)[None, :]
    cache_keys = prompt_keys.reshape(N_REQ, GROUPS_DEV, N_SEQ, PROMPT_DEV, KV, HD)
    cache_values = prompt_values.reshape(N_REQ, GROUPS_DEV, N_SEQ, PROMPT_DEV, KV, HD)
    pool_keys = tail_keys.reshape(N_REQ, N_SEQ, SLOTS * PAGE, KV, HD)
    pool_values = tail_values.reshape(N_REQ, N_SEQ, SLOTS * PAGE, KV, HD)
    pool_block = SLOTS * PAGE

    def one_block(block_index):
        keys_here = lax.dynamic_index_in_dim(cache_keys, block_index, 2, keepdims=False).astype(jnp.float32)
        values_here = lax.dynamic_index_in_dim(cache_values, block_index, 2, keepdims=False).astype(jnp.float32)
        pool_keys_here = lax.dynamic_index_in_dim(pool_keys, block_index, 1, keepdims=False).astype(jnp.float32)
        pool_values_here = lax.dynamic_index_in_dim(pool_values, block_index, 1, keepdims=False).astype(jnp.float32)
        prompt_pos = block_index * PROMPT_DEV + jnp.arange(PROMPT_DEV, dtype=jnp.int32)
        prompt_live = prompt_pos[None, None, :] < prompt_len[:, :, None]
        prompt_mask = (member[:, :, :, None] & prompt_live[:, None, :, :])[:, :, None, None, None, :, :]
        prompt_scores = jnp.einsum('rnskgd,rcpkd->rnskgcp', query_groups, keys_here)
        prompt_scores = jnp.where(prompt_mask, prompt_scores, NEGATIVE)
        owners_here = lax.dynamic_slice_in_dim(owners_rows, block_index * pool_block, pool_block, 1)
        positions_here = lax.dynamic_slice_in_dim(position_rows, block_index * pool_block, pool_block, 1)
        tail_mask = (owners_here[:, None, :] == jnp.arange(REQ_DEV, dtype=jnp.int32)[None, :, None]) & (positions_here[:, None, :] < tail_len[:, :, None])
        tail_mask = tail_mask[:, :, None, None, None, :]
        tail_scores = jnp.einsum('rnskgd,rpkd->rnskgp', query_groups, pool_keys_here)
        tail_scores = jnp.where(tail_mask, tail_scores, NEGATIVE)
        block_top = jnp.maximum(lax.optimization_barrier(jnp.max(prompt_scores, axis=(5, 6))), lax.optimization_barrier(jnp.max(tail_scores, axis=5)))
        prompt_probs = jnp.where(prompt_mask, jnp.exp(prompt_scores - block_top[..., None, None]), 0.0)
        tail_probs = jnp.where(tail_mask, jnp.exp(tail_scores - block_top[..., None]), 0.0)
        block_total = lax.optimization_barrier(jnp.sum(prompt_probs, axis=(5, 6))) + lax.optimization_barrier(jnp.sum(tail_probs, axis=5))
        prompt_round = prompt_probs.astype(jnp.bfloat16).astype(jnp.float32)
        tail_round = tail_probs.astype(jnp.bfloat16).astype(jnp.float32)
        block_accum = jnp.einsum('rnskgcp,rcpkd->rnskgd', prompt_round, values_here) + jnp.einsum('rnskgp,rpkd->rnskgd', tail_round, pool_values_here)
        return (block_top, block_total, block_accum)
    tops, totals, accums = lax.map(one_block, jnp.arange(N_SEQ, dtype=jnp.int32))
    keys_fresh = keys_new.reshape(N_REQ, REQ_DEV, STEPS, KV, HD).astype(jnp.float32)
    values_fresh = values_new.reshape(N_REQ, REQ_DEV, STEPS, KV, HD).astype(jnp.float32)
    new_scores = jnp.einsum('rnskgd,rnukd->rnskgu', query_groups, keys_fresh)
    causal = (jnp.arange(STEPS)[:, None] >= jnp.arange(STEPS)[None, :])[None, None, :, None, None, :]
    new_scores = jnp.where(causal, new_scores, NEGATIVE)
    highest = jnp.maximum(lax.optimization_barrier(jnp.max(tops, axis=0)), lax.optimization_barrier(jnp.max(new_scores, axis=5)))
    weights_blocks = jnp.exp(tops - highest[None])
    new_probs = jnp.where(causal, jnp.exp(new_scores - highest[..., None]), 0.0)
    total_sum = lax.optimization_barrier(jnp.sum(totals * weights_blocks, axis=0)) + lax.optimization_barrier(jnp.sum(new_probs, axis=5))
    accumulated = lax.optimization_barrier(jnp.sum(accums * weights_blocks[..., None], axis=0)) + jnp.einsum('rnskgu,rnukd->rnskgd', new_probs, values_fresh)
    attention = (accumulated / total_sum[..., None]).astype(jnp.bfloat16).reshape(REQUESTS * STEPS, H * HD)
    attn_out = jnp.dot(attention, w_out, preferred_element_type=jnp.float32)
    residual = hidden.reshape(REQUESTS * STEPS, D) + normalize(attn_out) * post_attn_gain
    ffn_in = (normalize(residual) * ffn_gain).astype(jnp.bfloat16)
    gate_out = jnp.dot(ffn_in, w_gate, preferred_element_type=jnp.float32)
    up_out = jnp.dot(ffn_in, w_up, preferred_element_type=jnp.float32)
    activated = (jax.nn.gelu(gate_out, approximate=True) * up_out).astype(jnp.bfloat16)
    down_out = jnp.dot(activated, w_down, preferred_element_type=jnp.float32)
    layer_out = residual + normalize(down_out) * post_ffn_gain
    return layer_out.astype(jnp.bfloat16).reshape(REQUESTS, STEPS, D)
```

```python
import jax
import jax.numpy as jnp
from jax import lax
from jax.experimental import pallas as pl
from jax.experimental.pallas import tpu as pltpu
from jax.sharding import PartitionSpec as P

MESH = pl.DeviceIdType.MESH
D = 2048
H = 8
KV = 2
HD = 256
PAGE = 16
QKV = 3072
NZ = 8
NY = 8
NS = 64
NR = 8
T = 64
STEPS = 4
REQS = 16
LANES = 128
DR = D // LANES
QR = QKV // LANES
EPSILON = 1e-06
NEGATIVE = -1e30
F32 = jnp.float32
BF16 = jnp.bfloat16
NT = (((1,), (1,)), ((), ()))


def iota(shape, dim):
    return lax.broadcasted_iota(jnp.int32, shape, dim)


def row_norm(row):
    total = jnp.sum(jnp.sum(row * row, axis=1, keepdims=True), axis=0, keepdims=True)
    return row * lax.rsqrt(total / D + EPSILON)


def kernel(
    hid_hbm, again_hbm, qgain_hbm, kgain_hbm, pagain_hbm, fgain_hbm, pfgain_hbm,
    wqkv_ref, wout_ref, wgate_ref, wup_ref, wdown_ref,
    pk_ref, pv_ref, tk_ref, tv_ref,
    grp_hbm, plen_hbm, tlen_hbm, table_hbm,
    out_ref,
    hid_ref, again_ref, qgain_ref, kgain_ref, pagain_ref, fgain_ref, pfgain_ref,
    grp_ref, plen_ref, tlen_ref, table_ref,
    hf, hid3, nb, kbuf, vbuf, maskf,
    wown, wq, wo, wg, wu, wd,
    psend, precv, qall, q2f,
    asend, arecv, of, orecv, xrow, xall, xf, x2,
    df, dsend, drecv, lrow, lall,
    local_sem, wq_s, wq_r, woy_s, woy_r, wor_s, wor_r, woc_s, woc_r, wf_s, wf_r, wfc_s, wfc_r,
    rs1_s, rs1_r, ag1_s, ag1_r, rs2_s, rs2_r, rs3_s, rs3_r,
    ag2_s, ag2_r, rs4_s, rs4_r, ag3_s, ag3_r,
):
    s = lax.axis_index("seq")
    r = lax.axis_index("req")
    z = s // NY
    y = s % NY
    token = y * NZ + z
    core = r % 2
    slot = core * 4 + r // 2
    sibling = (s, r + 1 - 2 * core)

    def seq_dev(zz, yy):
        return (zz * NY + yy, r)

    def req_dev(i):
        return (s, (r + i) % NR)

    rows_y = [(y + NY // 2 + k) % NY for k in range(NY)]

    def each_seq(fn):
        def line(i, carry):
            zz = (z + NZ // 2 + i) % NZ
            for yy in rows_y:
                fn(zz, yy)
            return carry

        lax.fori_loop(0, NZ // 2, line, 0)
        lax.fori_loop(NZ // 2 + 1, NZ, line, 0)
        for k, yy in enumerate(rows_y):
            if k != NY // 2:
                fn(z, yy)

    def copy(src, dst, ssem, rsem, dev):
        return pltpu.make_async_remote_copy(
            src_ref=src, dst_ref=dst, send_sem=ssem, recv_sem=rsem,
            device_id=dev, device_id_type=MESH,
        )

    def whole(ref, ssem, rsem):
        return copy(ref, ref, ssem, rsem, req_dev(1))

    pairs = [
        (hid_hbm, hid_ref),
        (again_hbm, again_ref),
        (wqkv_ref, wown),
        (wout_ref, wo.at[slot, pl.ds(y * 32, 32)]),
        (wgate_ref, wg.at[slot]),
        (wup_ref, wu.at[slot]),
        (wdown_ref, wd.at[slot]),
        (grp_hbm, grp_ref),
        (plen_hbm, plen_ref),
        (tlen_hbm, tlen_ref),
        (table_hbm, table_ref),
        (qgain_hbm, qgain_ref),
        (kgain_hbm, kgain_ref),
        (pagain_hbm, pagain_ref),
        (fgain_hbm, fgain_ref),
        (pfgain_hbm, pfgain_ref),
        (pk_ref.at[0], kbuf.at[pl.ds(0, 128)]),
        (pk_ref.at[1], kbuf.at[pl.ds(128, 128)]),
        (tk_ref.at[0], kbuf.at[pl.ds(256, 256)]),
        (pv_ref.at[0], vbuf.at[pl.ds(0, 128)]),
        (pv_ref.at[1], vbuf.at[pl.ds(128, 128)]),
        (tv_ref.at[0], vbuf.at[pl.ds(256, 256)]),
    ]
    loads = [pltpu.make_async_copy(a, b, local_sem.at[i]) for i, (a, b) in enumerate(pairs)]
    for ld in loads:
        ld.start()

    barrier = pltpu.get_barrier_semaphore()

    def greet(zz, yy):
        pl.semaphore_signal(barrier, inc=1, device_id=seq_dev(zz, yy), device_id_type=MESH)

    each_seq(greet)
    for i in range(1, NR):
        pl.semaphore_signal(barrier, inc=1, device_id=req_dev(i), device_id_type=MESH)

    def meet(dev):
        pl.semaphore_signal(barrier, inc=1, device_id=dev, device_id_type=MESH)

    for i in range(1, NR):
        meet((z * NY + r, (r + i) % NR))
        meet((z * NY + (y + i) % NY, y))
    pl.when(r != y)(lambda: meet((z * NY + r, r)))
    pl.when(r != y)(lambda: meet((s, y)))

    for ld in loads[:2]:
        ld.wait()
    for i in range(REQS):
        hf[STEPS * i : STEPS * (i + 1), :] = hid_ref[i].astype(F32)
    hidden = hf[...]
    scale = lax.rsqrt(jnp.mean(hidden * hidden, axis=1, keepdims=True) + EPSILON)
    nb[...] = (hidden * scale * again_ref[...]).astype(BF16)
    for j in range(DR):
        hid3[:, j, :] = hf[:, LANES * j : LANES * (j + 1)]

    peers = NS - 1 + NR - 1 + 2 * (NR - 1)
    pl.when(r == y)(lambda: pl.semaphore_wait(barrier, peers))
    pl.when(r != y)(lambda: pl.semaphore_wait(barrier, peers + 2))

    loads[2].wait()
    rows_here = wq.at[pl.ds(y * 32, 32)]
    for i in range(1, NR):
        copy(wown, rows_here, wq_s, wq_r, (z * NY + r, (r + i) % NR)).start()

    @pl.when(r != y)
    def _():
        copy(wown, rows_here, wq_s, wq_r, (z * NY + r, r)).start()

    @pl.when(r == y)
    def _():
        wq[pl.ds(pl.multiple_of(y * 32, 32), 32), :] = wown[...]

    x256 = nb[:, pl.ds(pl.multiple_of(z * 256, 256), 256)]

    @pl.when(r != y)
    def _():
        whole(wq, wq_s, wq_r).wait_recv()

    @pl.when(r == y)
    def _():
        whole(wq.at[pl.ds(0, 224)], wq_s, wq_r).wait_recv()

    part = jnp.dot(x256, wq[...], preferred_element_type=F32)
    for i in range(REQS):
        psend[i] = part[STEPS * i : STEPS * (i + 1), :]
    odd = y % 2
    quad = y // 2
    own_request = 2 * z + odd
    source = odd * NZ + z
    precv[source] = psend[own_request]
    for i in range(NZ):
        zz = (z + NZ // 2 + i) % NZ
        for b in range(2):
            if i == NZ // 2 and b == 0:
                continue
            other = (odd + b) % 2
            copy(
                psend.at[2 * zz + other], precv.at[source], rs1_s, rs1_r,
                seq_dev(zz, 2 * quad + other),
            ).start()

    def over_x(w, ssem, rsem):
        for i in range(1, 4):
            copy(w.at[slot], w.at[slot], ssem, rsem, (s, (r + 2 * i) % NR)).start()

    def over_core(w, ssem, rsem):
        half = w.at[pl.ds(core * 4, 4)]
        copy(half, half, ssem, rsem, sibling).start()

    for ld in loads[3:7]:
        ld.wait()
    mine = wo.at[slot, pl.ds(y * 32, 32)]
    for i in range(1, NY):
        copy(mine, mine, woy_s, woy_r, seq_dev(z, (y + i) % NY)).start()
    over_x(wg, wf_s.at[0], wf_r.at[0])

    for ld in loads[7:16]:
        ld.wait()
    req_of = iota((T, REQS), 0) // STEPS == iota((T, REQS), 1)
    group = jnp.sum(
        jnp.where(req_of, (grp_ref[...] % 2).astype(F32), 0.0), axis=1, keepdims=True
    )
    tail_len = jnp.sum(jnp.where(req_of, tlen_ref[...].astype(F32), 0.0), axis=1, keepdims=True)
    lanes = iota((T, 256), 1)
    plen = jnp.where(lanes < 128, plen_ref[:, 0:1], plen_ref[:, 1:2])
    prompt_live = (s * 128 + lanes % 128 < plen) & (group == (lanes // 128).astype(F32))
    match = (table_ref[...] == s * 16 + iota((256, 1024), 0) // PAGE).astype(F32).astype(BF16)
    entry = iota((8, 1024), 1)
    digits = jnp.where(iota((8, 1024), 0) == 0, entry // 64, entry % 64)
    found = lax.dot_general(
        digits.astype(F32).astype(BF16), match, NT, preferred_element_type=F32
    )
    owner = found[0:1, :]
    position = found[1:2, :] * PAGE + (iota((1, 256), 1) % PAGE).astype(F32)
    own_req = (iota((T, 256), 0) // STEPS).astype(F32)
    tail_live = (owner == own_req) & (position < tail_len)
    maskf[:, 0:256] = jnp.where(prompt_live, 1.0, 0.0)
    maskf[:, 256:512] = jnp.where(tail_live, 1.0, 0.0)

    whole(precv.at[pl.ds(0, REQS - 1)], rs1_s, rs1_r).wait_recv()
    low = jnp.sum(precv[0:NZ], axis=0)
    high = jnp.sum(precv[NZ : 2 * NZ], axis=0)
    chunks = [low[:, LANES * u : LANES * (u + 1)] for u in range(3)]
    chunks += [high[:, LANES * u : LANES * (u + 1)] for u in range(3)]
    pieces = []
    for i in range(3):
        pair = chunks[2 * i : 2 * i + 2]
        mean = sum(jnp.sum(c * c, axis=1, keepdims=True) for c in pair) / HD
        inverse = lax.rsqrt(mean + EPSILON)
        head = 3 * quad + i
        for u in range(2):
            gain = jnp.where(
                head < H,
                qgain_ref[u : u + 1, :],
                jnp.where(head < H + KV, kgain_ref[u : u + 1, :], 1.0),
            )
            pieces.append(pair[u] * inverse * gain)
    place = own_request * 4 + quad
    qall[place] = jnp.concatenate(pieces, axis=1).astype(BF16)

    def send_ag1(zz, yy):
        copy(qall.at[place], qall.at[place], ag1_s, ag1_r, seq_dev(zz, yy)).start()

    each_seq(send_ag1)
    whole(wo.at[0, pl.ds(0, 224)], woy_s, woy_r).wait_recv()
    over_x(wo, wor_s, wor_r)
    over_x(wu, wf_s.at[1], wf_r.at[1])
    over_x(wd, wf_s.at[2], wf_r.at[2])
    for ld in loads[16:]:
        ld.wait()
    whole(qall.at[pl.ds(0, NS - 1)], ag1_s, ag1_r).wait_recv()
    for i in range(REQS):
        for k in range(4):
            block = qall[4 * i + k].astype(F32)
            for u in range(3):
                top = T * (3 * k + u) + STEPS * i
                q2f[top : top + STEPS, :] = block[:, HD * u : HD * (u + 1)]

    mask = maskf[...]
    mask4 = jnp.concatenate([mask, mask, mask, mask], axis=0) > 0.5
    rows = H // KV * T
    for c in range(KV):
        heads = q2f[rows * c : rows * (c + 1), :].astype(BF16)
        scores = lax.dot_general(
            heads, kbuf[:, HD * c : HD * (c + 1)], NT, preferred_element_type=F32
        )
        scores = jnp.where(mask4, scores, NEGATIVE)
        top = jnp.max(scores, axis=1, keepdims=True)
        probs = jnp.where(mask4, jnp.exp(scores - top), 0.0)
        total = jnp.sum(probs, axis=1, keepdims=True)
        accum = jnp.dot(
            probs.astype(BF16), vbuf[:, HD * c : HD * (c + 1)], preferred_element_type=F32
        )
        lane = iota((rows, LANES), 1)
        stats = jnp.zeros((rows, LANES), F32)
        for base, rest in ((0, top), (3, total)):
            for k in range(3):
                high = rest.astype(BF16).astype(F32)
                stats = jnp.where(lane == base + k, high, stats)
                rest = rest - high
        eight = rows // 8
        asend[eight * c : eight * (c + 1), :, 0:HD] = accum.reshape(eight, 8, HD).astype(BF16)
        asend[eight * c : eight * (c + 1), :, HD : HD + LANES] = stats.reshape(
            eight, 8, LANES
        ).astype(BF16)

    arecv[s] = asend[s]

    def send_rs2(zz, yy):
        copy(asend.at[zz * NY + yy], arecv.at[s], rs2_s, rs2_r, seq_dev(zz, yy)).start()

    each_seq(send_rs2)
    whole(wo.at[pl.ds(0, 3)], wor_s, wor_r).wait_recv()
    over_core(wo, woc_s, woc_r)
    for k, w in enumerate((wg, wu, wd)):
        whole(w.at[pl.ds(0, 3)], wf_s.at[k], wf_r.at[k]).wait_recv()
        over_core(w, wfc_s.at[k], wfc_r.at[k])

    def eight_of(head):
        return q2f[pl.ds(pl.multiple_of(head * T + y * 8, 8), 8), :]

    q8 = eight_of(z).astype(BF16)
    k8 = eight_of(H + z // 4).astype(BF16)
    v8 = eight_of(H + KV + z // 4)
    new_scores = lax.dot_general(q8, k8, NT, preferred_element_type=F32)
    qi = iota((8, 8), 0)
    ki = iota((8, 8), 1)
    causal = (qi // STEPS == ki // STEPS) & (ki <= qi)
    new_scores = jnp.where(causal, new_scores, NEGATIVE)
    new_top = jnp.max(new_scores, axis=1, keepdims=True)

    whole(arecv.at[pl.ds(0, NS - 1)], rs2_s, rs2_r).wait_recv()
    stats = arecv[:, :, HD : HD + LANES].astype(F32)
    tops = stats[:, :, 0:1] + stats[:, :, 1:2] + stats[:, :, 2:3]
    totals = stats[:, :, 3:4] + stats[:, :, 4:5] + stats[:, :, 5:6]
    highest = jnp.maximum(jnp.max(tops, axis=0), new_top)
    weight = jnp.exp(tops - highest[None])
    new_probs = jnp.where(causal, jnp.exp(new_scores - highest), 0.0)
    denominator = jnp.sum(totals * weight, axis=0) + jnp.sum(new_probs, axis=1, keepdims=True)
    numerator = jnp.sum(arecv[:, :, 0:HD].astype(F32) * weight, axis=0) + jnp.dot(
        new_probs, v8, preferred_element_type=F32, precision=lax.Precision.HIGHEST
    )
    attention = (numerator / denominator).astype(BF16)

    whole(wo.at[pl.ds(0, 4)], woc_s, woc_r).wait_recv()
    for k in range(NR):
        part = jnp.dot(attention, wo[k % 2 * 4 + k // 2], preferred_element_type=F32)
        for u in range(2):
            of[:, 2 * k + u, :] = part[:, LANES * u : LANES * (u + 1)]
    orecv[z] = of[z]
    for i in range(1, NZ):
        zz = (z + i) % NZ
        copy(of.at[zz], orecv.at[z], rs3_s, rs3_r, seq_dev(zz, y)).start()
    whole(orecv.at[pl.ds(0, NZ - 1)], rs3_s, rs3_r).wait_recv()
    out_row = jnp.sum(orecv[...], axis=0)
    residual = hid3[token] + row_norm(out_row) * pagain_ref[...]
    xrow[...] = (row_norm(residual) * fgain_ref[...]).astype(BF16)
    xall[token] = xrow[...]

    def send_ag2(zz, yy):
        copy(xrow, xall.at[token], ag2_s, ag2_r, seq_dev(zz, yy)).start()

    each_seq(send_ag2)
    for k, w in enumerate((wg, wu, wd)):
        whole(w.at[pl.ds(0, 4)], wfc_s.at[k], wfc_r.at[k]).wait_recv()
    whole(xall.at[pl.ds(0, NS - 1)], ag2_s, ag2_r).wait_recv()

    xf[...] = xall[...].astype(F32)
    for j in range(DR):
        x2[:, LANES * j : LANES * (j + 1)] = xf[:, j, :].astype(BF16)
    gate = jnp.zeros((T, LANES), F32)
    up = jnp.zeros((T, LANES), F32)
    for k in range(NR):
        xk = x2[:, 256 * k : 256 * (k + 1)]
        gate = gate + jnp.dot(xk, wg[k % 2 * 4 + k // 2], preferred_element_type=F32)
        up = up + jnp.dot(xk, wu[k % 2 * 4 + k // 2], preferred_element_type=F32)
    activated = (jax.nn.gelu(gate, approximate=True) * up).astype(BF16)
    for k in range(NR):
        part = jnp.dot(activated, wd[k % 2 * 4 + k // 2], preferred_element_type=F32)
        for u in range(2):
            df[:, 2 * k + u, :] = part[:, LANES * u : LANES * (u + 1)]
    dsend[...] = df[...].astype(BF16)
    drecv[s] = dsend[token]

    def send_rs4(zz, yy):
        copy(dsend.at[yy * NZ + zz], drecv.at[s], rs4_s, rs4_r, seq_dev(zz, yy)).start()

    each_seq(send_rs4)
    whole(drecv.at[pl.ds(0, NS - 1)], rs4_s, rs4_r).wait_recv()
    down = jnp.sum(drecv[...].astype(F32), axis=0)
    lrow[...] = (residual + row_norm(down) * pfgain_ref[...]).astype(BF16)
    lall[token] = lrow[...]

    def send_ag3(zz, yy):
        copy(lrow, lall.at[token], ag3_s, ag3_r, seq_dev(zz, yy)).start()

    each_seq(send_ag3)

    whole(wq.at[pl.ds(0, 224)], wq_s, wq_r).wait_send()
    pl.when(r != y)(lambda: whole(wq.at[pl.ds(0, 32)], wq_s, wq_r).wait_send())
    whole(wo.at[0, pl.ds(0, 224)], woy_s, woy_r).wait_send()
    whole(wo.at[pl.ds(0, 3)], wor_s, wor_r).wait_send()
    whole(wo.at[pl.ds(0, 4)], woc_s, woc_r).wait_send()
    for k, w in enumerate((wg, wu, wd)):
        whole(w.at[pl.ds(0, 3)], wf_s.at[k], wf_r.at[k]).wait_send()
        whole(w.at[pl.ds(0, 4)], wfc_s.at[k], wfc_r.at[k]).wait_send()
    whole(precv.at[pl.ds(0, REQS - 1)], rs1_s, rs1_r).wait_send()
    whole(qall.at[pl.ds(0, NS - 1)], ag1_s, ag1_r).wait_send()
    whole(arecv.at[pl.ds(0, NS - 1)], rs2_s, rs2_r).wait_send()
    whole(orecv.at[pl.ds(0, NZ - 1)], rs3_s, rs3_r).wait_send()
    whole(xall.at[pl.ds(0, NS - 1)], ag2_s, ag2_r).wait_send()
    whole(drecv.at[pl.ds(0, NS - 1)], rs4_s, rs4_r).wait_send()

    whole(lall.at[pl.ds(0, NS - 1)], ag3_s, ag3_r).wait_recv()
    xf[...] = lall[...].astype(F32)
    for j in range(DR):
        out_ref[:, LANES * j : LANES * (j + 1)] = xf[:, j, :].astype(BF16)
    whole(lall.at[pl.ds(0, NS - 1)], ag3_s, ag3_r).wait_send()


def on_device(
    hidden_in, attn_gain, q_gain, k_gain, post_attn_gain, ffn_gain, post_ffn_gain,
    w_qkv, w_out, w_gate, w_up, w_down,
    prompt_keys, prompt_values, tail_keys, tail_values,
    group_of, prompt_lengths, tail_lengths, page_table,
):
    vmem = pl.BlockSpec(memory_space=pltpu.VMEM)
    hbm = pl.BlockSpec(memory_space=pltpu.HBM)
    dma = pltpu.SemaphoreType.DMA
    scratch = [
        pltpu.VMEM((REQS, STEPS, D), BF16),
        pltpu.VMEM((1, D), F32),
        pltpu.VMEM((2, LANES), F32),
        pltpu.VMEM((2, LANES), F32),
        pltpu.VMEM((DR, LANES), F32),
        pltpu.VMEM((DR, LANES), F32),
        pltpu.VMEM((DR, LANES), F32),
        pltpu.VMEM((1, REQS), jnp.int32),
        pltpu.VMEM((1, 2), jnp.int32),
        pltpu.VMEM((1, REQS), jnp.int32),
        pltpu.VMEM((1, 1024), jnp.int32),
        pltpu.VMEM((T, D), F32),
        pltpu.VMEM((T, DR, LANES), F32),
        pltpu.VMEM((T, D), BF16),
        pltpu.VMEM((512, 512), BF16),
        pltpu.VMEM((512, 512), BF16),
        pltpu.VMEM((T, 512), F32),
        pltpu.VMEM((32, 384), BF16),
        pltpu.VMEM((256, 384), BF16),
        pltpu.VMEM((NR, 256, 256), BF16),
        pltpu.VMEM((NR, 256, LANES), BF16),
        pltpu.VMEM((NR, 256, LANES), BF16),
        pltpu.VMEM((NR, LANES, 256), BF16),
        pltpu.VMEM((REQS, STEPS, 384), F32),
        pltpu.VMEM((REQS, STEPS, 384), F32),
        pltpu.VMEM((NS, STEPS, 768), BF16),
        pltpu.VMEM((12 * T, HD), F32),
        pltpu.VMEM((NS, 8, HD + LANES), BF16),
        pltpu.VMEM((NS, 8, HD + LANES), BF16),
        pltpu.VMEM((NZ, DR, LANES), F32),
        pltpu.VMEM((NZ, DR, LANES), F32),
        pltpu.VMEM((DR, LANES), BF16),
        pltpu.VMEM((T, DR, LANES), BF16),
        pltpu.VMEM((T, DR, LANES), F32),
        pltpu.VMEM((T, D), BF16),
        pltpu.VMEM((T, DR, LANES), F32),
        pltpu.VMEM((T, DR, LANES), BF16),
        pltpu.VMEM((NS, DR, LANES), BF16),
        pltpu.VMEM((DR, LANES), BF16),
        pltpu.VMEM((T, DR, LANES), BF16),
        dma((22,)),
        dma, dma, dma, dma, dma, dma, dma, dma, dma((3,)), dma((3,)), dma((3,)), dma((3,)),
        dma, dma, dma, dma, dma, dma, dma, dma,
        dma, dma, dma, dma, dma, dma,
    ]
    out = pl.pallas_call(
        kernel,
        name="decode_layer",
        out_shape=jax.ShapeDtypeStruct((T, D), BF16),
        in_specs=[hbm] * 20,
        out_specs=vmem,
        scratch_shapes=scratch,
        compiler_params=pltpu.CompilerParams(
            collective_id=0, has_side_effects=True, vmem_limit_bytes=40 << 20
        ),
    )(*[pltpu.with_memory_space_constraint(a, pltpu.HBM) for a in (
        hidden_in,
        attn_gain.reshape(1, D),
        q_gain.reshape(2, LANES),
        k_gain.reshape(2, LANES),
        post_attn_gain.reshape(DR, LANES),
        ffn_gain.reshape(DR, LANES),
        post_ffn_gain.reshape(DR, LANES),
        w_qkv, w_out, w_gate, w_up, w_down,
        prompt_keys, prompt_values, tail_keys, tail_values,
        group_of.reshape(1, REQS),
        prompt_lengths.reshape(1, 2),
        tail_lengths.reshape(1, REQS),
        page_table,
    )])
    return out.reshape(REQS, STEPS, D)


def solution(mesh):
    return jax.shard_map(
        on_device,
        mesh=mesh,
        in_specs=(
            P("req", None, None),
            P(), P(), P(), P(), P(), P(),
            P("seq", "req"),
            P("seq", "req"),
            P("req", "seq"),
            P("req", "seq"),
            P("seq", "req"),
            P("req", "seq", None),
            P("req", "seq", None),
            P("req", "seq", None),
            P("req", "seq", None),
            P("req"), P("req"), P("req"),
            P("req", None),
        ),
        out_specs=P("req", None, None),
        check_vma=False,
    )
```

```python
import jax
import jax.numpy as jnp
from jax import lax
from jax.experimental import pallas as pl
from jax.experimental.pallas import tpu as pltpu
from jax.sharding import PartitionSpec as P

MESH = pl.DeviceIdType.MESH
D = 2048
H = 8
KV = 2
HD = 256
PAGE = 16
QKV = 3072
NZ = 8
NY = 8
NS = 64
NR = 8
T = 64
STEPS = 4
REQS = 16
LANES = 128
DR = D // LANES
QR = QKV // LANES
EPSILON = 1e-06
NEGATIVE = -1e30
F32 = jnp.float32
BF16 = jnp.bfloat16
NT = (((1,), (1,)), ((), ()))


def iota(shape, dim):
    return lax.broadcasted_iota(jnp.int32, shape, dim)


def row_norm(row):
    total = jnp.sum(jnp.sum(row * row, axis=1, keepdims=True), axis=0, keepdims=True)
    return row * lax.rsqrt(total / D + EPSILON)


def kernel(
    hid_hbm, again_hbm, qgain_hbm, kgain_hbm, pagain_hbm, fgain_hbm, pfgain_hbm,
    wqkv_ref, wout_ref, wgate_ref, wup_ref, wdown_ref,
    pk_ref, pv_ref, tk_ref, tv_ref,
    grp_hbm, plen_hbm, tlen_hbm, table_hbm,
    out_ref,
    hid_ref, again_ref, qgain_ref, kgain_ref, pagain_ref, fgain_ref, pfgain_ref,
    grp_ref, plen_ref, tlen_ref, table_ref,
    hf, hid3, nb, kbuf, vbuf, maskf,
    wown, wq, wo, wg, wu, wd,
    psend, precv, qall, q2f,
    asend, arecv, of, orecv, xrow, xall, xf, x2,
    df, dsend, drecv, lrow, lall,
    local_sem, wq_s, wq_r, woy_s, woy_r, wor_s, wor_r, woc_s, woc_r, wf_s, wf_r, wfc_s, wfc_r,
    rs1_s, rs1_r, ag1_s, ag1_r, rs2_s, rs2_r, rs3_s, rs3_r,
    ag2_s, ag2_r, rs4_s, rs4_r, ag3_s, ag3_r,
):
    s = lax.axis_index("seq")
    r = lax.axis_index("req")
    z = s // NY
    y = s % NY
    token = y * NZ + z
    chunk = (y + r) % NY
    core = r % 2
    slot = core * 4 + r // 2
    sibling = (s, r + 1 - 2 * core)

    def seq_dev(zz, yy):
        return (zz * NY + yy, r)

    def req_dev(i):
        return (s, (r + i) % NR)

    rows_y = [(y + NY // 2 + k) % NY for k in range(NY)]

    def each_seq(fn):
        def line(i, carry):
            zz = (z + NZ // 2 + i) % NZ
            for yy in rows_y:
                fn(zz, yy)
            return carry

        lax.fori_loop(0, NZ // 2, line, 0)
        lax.fori_loop(NZ // 2 + 1, NZ, line, 0)
        for k, yy in enumerate(rows_y):
            if k != NY // 2:
                fn(z, yy)

    def copy(src, dst, ssem, rsem, dev):
        return pltpu.make_async_remote_copy(
            src_ref=src, dst_ref=dst, send_sem=ssem, recv_sem=rsem,
            device_id=dev, device_id_type=MESH,
        )

    def whole(ref, ssem, rsem):
        return copy(ref, ref, ssem, rsem, req_dev(1))

    pairs = [
        (hid_hbm, hid_ref),
        (again_hbm, again_ref),
        (wqkv_ref, wown),
        (wout_ref, wo.at[slot, pl.ds(y * 32, 32)]),
        (wgate_ref, wg.at[slot]),
        (wup_ref, wu.at[slot]),
        (wdown_ref, wd.at[slot]),
        (grp_hbm, grp_ref),
        (plen_hbm, plen_ref),
        (tlen_hbm, tlen_ref),
        (table_hbm, table_ref),
        (qgain_hbm, qgain_ref),
        (kgain_hbm, kgain_ref),
        (pagain_hbm, pagain_ref),
        (fgain_hbm, fgain_ref),
        (pfgain_hbm, pfgain_ref),
        (pk_ref.at[0], kbuf.at[pl.ds(0, 128)]),
        (pk_ref.at[1], kbuf.at[pl.ds(128, 128)]),
        (tk_ref.at[0], kbuf.at[pl.ds(256, 256)]),
        (pv_ref.at[0], vbuf.at[pl.ds(0, 128)]),
        (pv_ref.at[1], vbuf.at[pl.ds(128, 128)]),
        (tv_ref.at[0], vbuf.at[pl.ds(256, 256)]),
    ]
    loads = [pltpu.make_async_copy(a, b, local_sem.at[i]) for i, (a, b) in enumerate(pairs)]
    for ld in loads:
        ld.start()

    barrier = pltpu.get_barrier_semaphore()

    def meet(dev):
        pl.semaphore_signal(barrier, inc=1, device_id=dev, device_id_type=MESH)

    partner = (chunk + 1 - 2 * (chunk % 2) + NR - r) % NY
    for i in range(1, NY):
        meet(seq_dev(z, (y + i) % NY))
        meet(seq_dev((z + i) % NZ, y))
    for i in range(NZ):
        meet(seq_dev((z + i) % NZ, partner))
    for i in range(1, 4):
        meet((s, (r + 2 * i) % NR))
    meet(sibling)

    for i in range(1, NR):
        meet((z * NY + NY - i, (r + i) % NR))
        meet((z * NY + (y + i) % NY, chunk))
    pl.when(y != 0)(lambda: meet((z * NY, r)))
    pl.when(y != 0)(lambda: meet((s, chunk)))

    for ld in loads[:2]:
        ld.wait()
    for i in range(REQS):
        hf[STEPS * i : STEPS * (i + 1), :] = hid_ref[i].astype(F32)
    hidden = hf[...]
    scale = lax.rsqrt(jnp.mean(hidden * hidden, axis=1, keepdims=True) + EPSILON)
    nb[...] = (hidden * scale * again_ref[...]).astype(BF16)
    for j in range(DR):
        hid3[:, j, :] = hf[:, LANES * j : LANES * (j + 1)]

    peers = 2 * (NY - 1) + NZ + 4 + 2 * (NR - 1)
    pl.when(y == 0)(lambda: pl.semaphore_wait(barrier, peers))
    pl.when(y != 0)(lambda: pl.semaphore_wait(barrier, peers + 2))

    loads[2].wait()
    rows_here = wq.at[pl.ds(y * 32, 32)]
    for i in range(1, NR):
        copy(wown, rows_here, wq_s, wq_r, (z * NY + NY - i, (r + i) % NR)).start()

    @pl.when(y != 0)
    def _():
        copy(wown, rows_here, wq_s, wq_r, (z * NY, r)).start()

    @pl.when(y == 0)
    def _():
        wq[pl.ds(pl.multiple_of(y * 32, 32), 32), :] = wown[...]

    x256 = nb[:, pl.ds(pl.multiple_of(z * 256, 256), 256)]

    @pl.when(y != 0)
    def _():
        whole(wq, wq_s, wq_r).wait_recv()

    @pl.when(y == 0)
    def _():
        whole(wq.at[pl.ds(0, 224)], wq_s, wq_r).wait_recv()

    part = jnp.dot(x256, wq[...], preferred_element_type=F32)
    for i in range(REQS):
        psend[i] = part[STEPS * i : STEPS * (i + 1), :]
    odd = chunk % 2
    quad = chunk // 2
    own_request = 2 * z + odd
    source = odd * NZ + z
    precv[source] = psend[own_request]
    for i in range(NZ):
        zz = (z + NZ // 2 + i) % NZ
        for b in range(2):
            if i == NZ // 2 and b == 0:
                continue
            other = (odd + b) % 2
            copy(
                psend.at[2 * zz + other], precv.at[source], rs1_s, rs1_r,
                seq_dev(zz, (2 * quad + other + NR - r) % NY),
            ).start()

    def over_x(w, ssem, rsem):
        for i in range(1, 4):
            copy(w.at[slot], w.at[slot], ssem, rsem, (s, (r + 2 * i) % NR)).start()

    def over_core(w, ssem, rsem):
        half = w.at[pl.ds(core * 4, 4)]
        copy(half, half, ssem, rsem, sibling).start()

    for ld in loads[3:7]:
        ld.wait()
    mine = wo.at[slot, pl.ds(y * 32, 32)]
    for i in range(1, NY):
        copy(mine, mine, woy_s, woy_r, seq_dev(z, (y + i) % NY)).start()
    over_x(wg, wf_s.at[0], wf_r.at[0])

    for ld in loads[7:16]:
        ld.wait()
    req_of = iota((T, REQS), 0) // STEPS == iota((T, REQS), 1)
    group = jnp.sum(
        jnp.where(req_of, (grp_ref[...] % 2).astype(F32), 0.0), axis=1, keepdims=True
    )
    tail_len = jnp.sum(jnp.where(req_of, tlen_ref[...].astype(F32), 0.0), axis=1, keepdims=True)
    lanes = iota((T, 256), 1)
    plen = jnp.where(lanes < 128, plen_ref[:, 0:1], plen_ref[:, 1:2])
    prompt_live = (s * 128 + lanes % 128 < plen) & (group == (lanes // 128).astype(F32))
    match = (table_ref[...] == s * 16 + iota((256, 1024), 0) // PAGE).astype(F32).astype(BF16)
    entry = iota((8, 1024), 1)
    digits = jnp.where(iota((8, 1024), 0) == 0, entry // 64, entry % 64)
    found = lax.dot_general(
        digits.astype(F32).astype(BF16), match, NT, preferred_element_type=F32
    )
    owner = found[0:1, :]
    position = found[1:2, :] * PAGE + (iota((1, 256), 1) % PAGE).astype(F32)
    own_req = (iota((T, 256), 0) // STEPS).astype(F32)
    tail_live = (owner == own_req) & (position < tail_len)
    maskf[:, 0:256] = jnp.where(prompt_live, 1.0, 0.0)
    maskf[:, 256:512] = jnp.where(tail_live, 1.0, 0.0)

    whole(precv.at[pl.ds(0, REQS - 1)], rs1_s, rs1_r).wait_recv()
    low = jnp.sum(precv[0:NZ], axis=0)
    high = jnp.sum(precv[NZ : 2 * NZ], axis=0)
    chunks = [low[:, LANES * u : LANES * (u + 1)] for u in range(3)]
    chunks += [high[:, LANES * u : LANES * (u + 1)] for u in range(3)]
    pieces = []
    for i in range(3):
        pair = chunks[2 * i : 2 * i + 2]
        mean = sum(jnp.sum(c * c, axis=1, keepdims=True) for c in pair) / HD
        inverse = lax.rsqrt(mean + EPSILON)
        head = 3 * quad + i
        for u in range(2):
            gain = jnp.where(
                head < H,
                qgain_ref[u : u + 1, :],
                jnp.where(head < H + KV, kgain_ref[u : u + 1, :], 1.0),
            )
            pieces.append(pair[u] * inverse * gain)
    place = own_request * 4 + quad
    qall[place] = jnp.concatenate(pieces, axis=1).astype(BF16)

    def send_ag1(zz, yy):
        copy(qall.at[place], qall.at[place], ag1_s, ag1_r, seq_dev(zz, yy)).start()

    each_seq(send_ag1)
    whole(wo.at[0, pl.ds(0, 224)], woy_s, woy_r).wait_recv()
    over_x(wo, wor_s, wor_r)
    over_x(wu, wf_s.at[1], wf_r.at[1])
    over_x(wd, wf_s.at[2], wf_r.at[2])
    for ld in loads[16:]:
        ld.wait()
    whole(qall.at[pl.ds(0, NS - 1)], ag1_s, ag1_r).wait_recv()
    for i in range(REQS):
        for k in range(4):
            block = qall[4 * i + k].astype(F32)
            for u in range(3):
                top = T * (3 * k + u) + STEPS * i
                q2f[top : top + STEPS, :] = block[:, HD * u : HD * (u + 1)]

    mask = maskf[...]
    mask4 = jnp.concatenate([mask, mask, mask, mask], axis=0) > 0.5
    rows = H // KV * T
    for c in range(KV):
        heads = q2f[rows * c : rows * (c + 1), :].astype(BF16)
        scores = lax.dot_general(
            heads, kbuf[:, HD * c : HD * (c + 1)], NT, preferred_element_type=F32
        )
        scores = jnp.where(mask4, scores, NEGATIVE)
        top = jnp.max(scores, axis=1, keepdims=True)
        probs = jnp.where(mask4, jnp.exp(scores - top), 0.0)
        total = jnp.sum(probs, axis=1, keepdims=True)
        accum = jnp.dot(
            probs.astype(BF16), vbuf[:, HD * c : HD * (c + 1)], preferred_element_type=F32
        )
        lane = iota((rows, LANES), 1)
        stats = jnp.zeros((rows, LANES), F32)
        for base, rest in ((0, top), (3, total)):
            for k in range(3):
                high = rest.astype(BF16).astype(F32)
                stats = jnp.where(lane == base + k, high, stats)
                rest = rest - high
        eight = rows // 8
        asend[eight * c : eight * (c + 1), :, 0:HD] = accum.reshape(eight, 8, HD).astype(BF16)
        asend[eight * c : eight * (c + 1), :, HD : HD + LANES] = stats.reshape(
            eight, 8, LANES
        ).astype(BF16)

    arecv[s] = asend[s]

    def send_rs2(zz, yy):
        copy(asend.at[zz * NY + yy], arecv.at[s], rs2_s, rs2_r, seq_dev(zz, yy)).start()

    each_seq(send_rs2)
    whole(wo.at[pl.ds(0, 3)], wor_s, wor_r).wait_recv()
    over_core(wo, woc_s, woc_r)
    for k, w in enumerate((wg, wu, wd)):
        whole(w.at[pl.ds(0, 3)], wf_s.at[k], wf_r.at[k]).wait_recv()
        over_core(w, wfc_s.at[k], wfc_r.at[k])

    def eight_of(head):
        return q2f[pl.ds(pl.multiple_of(head * T + y * 8, 8), 8), :]

    q8 = eight_of(z).astype(BF16)
    k8 = eight_of(H + z // 4).astype(BF16)
    v8 = eight_of(H + KV + z // 4)
    new_scores = lax.dot_general(q8, k8, NT, preferred_element_type=F32)
    qi = iota((8, 8), 0)
    ki = iota((8, 8), 1)
    causal = (qi // STEPS == ki // STEPS) & (ki <= qi)
    new_scores = jnp.where(causal, new_scores, NEGATIVE)
    new_top = jnp.max(new_scores, axis=1, keepdims=True)

    whole(arecv.at[pl.ds(0, NS - 1)], rs2_s, rs2_r).wait_recv()
    stats = arecv[:, :, HD : HD + LANES].astype(F32)
    tops = stats[:, :, 0:1] + stats[:, :, 1:2] + stats[:, :, 2:3]
    totals = stats[:, :, 3:4] + stats[:, :, 4:5] + stats[:, :, 5:6]
    highest = jnp.maximum(jnp.max(tops, axis=0), new_top)
    weight = jnp.exp(tops - highest[None])
    new_probs = jnp.where(causal, jnp.exp(new_scores - highest), 0.0)
    denominator = jnp.sum(totals * weight, axis=0) + jnp.sum(new_probs, axis=1, keepdims=True)
    numerator = jnp.sum(arecv[:, :, 0:HD].astype(F32) * weight, axis=0) + jnp.dot(
        new_probs, v8, preferred_element_type=F32, precision=lax.Precision.HIGHEST
    )
    attention = (numerator / denominator).astype(BF16)

    whole(wo.at[pl.ds(0, 4)], woc_s, woc_r).wait_recv()
    for k in range(NR):
        part = jnp.dot(attention, wo[k % 2 * 4 + k // 2], preferred_element_type=F32)
        for u in range(2):
            of[:, 2 * k + u, :] = part[:, LANES * u : LANES * (u + 1)]
    orecv[z] = of[z]
    for i in range(1, NZ):
        zz = (z + i) % NZ
        copy(of.at[zz], orecv.at[z], rs3_s, rs3_r, seq_dev(zz, y)).start()
    whole(orecv.at[pl.ds(0, NZ - 1)], rs3_s, rs3_r).wait_recv()
    out_row = jnp.sum(orecv[...], axis=0)
    residual = hid3[token] + row_norm(out_row) * pagain_ref[...]
    xrow[...] = (row_norm(residual) * fgain_ref[...]).astype(BF16)
    xall[token] = xrow[...]

    def send_ag2(zz, yy):
        copy(xrow, xall.at[token], ag2_s, ag2_r, seq_dev(zz, yy)).start()

    each_seq(send_ag2)
    for k, w in enumerate((wg, wu, wd)):
        whole(w.at[pl.ds(0, 4)], wfc_s.at[k], wfc_r.at[k]).wait_recv()
    whole(xall.at[pl.ds(0, NS - 1)], ag2_s, ag2_r).wait_recv()

    xf[...] = xall[...].astype(F32)
    for j in range(DR):
        x2[:, LANES * j : LANES * (j + 1)] = xf[:, j, :].astype(BF16)
    gate = jnp.zeros((T, LANES), F32)
    up = jnp.zeros((T, LANES), F32)
    for k in range(NR):
        xk = x2[:, 256 * k : 256 * (k + 1)]
        gate = gate + jnp.dot(xk, wg[k % 2 * 4 + k // 2], preferred_element_type=F32)
        up = up + jnp.dot(xk, wu[k % 2 * 4 + k // 2], preferred_element_type=F32)
    activated = (jax.nn.gelu(gate, approximate=True) * up).astype(BF16)
    for k in range(NR):
        part = jnp.dot(activated, wd[k % 2 * 4 + k // 2], preferred_element_type=F32)
        for u in range(2):
            df[:, 2 * k + u, :] = part[:, LANES * u : LANES * (u + 1)]
    dsend[...] = df[...].astype(BF16)
    drecv[s] = dsend[token]

    def send_rs4(zz, yy):
        copy(dsend.at[yy * NZ + zz], drecv.at[s], rs4_s, rs4_r, seq_dev(zz, yy)).start()

    each_seq(send_rs4)
    whole(drecv.at[pl.ds(0, NS - 1)], rs4_s, rs4_r).wait_recv()
    down = jnp.sum(drecv[...].astype(F32), axis=0)
    lrow[...] = (residual + row_norm(down) * pfgain_ref[...]).astype(BF16)
    lall[token] = lrow[...]

    def send_ag3(zz, yy):
        copy(lrow, lall.at[token], ag3_s, ag3_r, seq_dev(zz, yy)).start()

    each_seq(send_ag3)

    whole(wq.at[pl.ds(0, 224)], wq_s, wq_r).wait_send()
    pl.when(y != 0)(lambda: whole(wq.at[pl.ds(0, 32)], wq_s, wq_r).wait_send())
    whole(wo.at[0, pl.ds(0, 224)], woy_s, woy_r).wait_send()
    whole(wo.at[pl.ds(0, 3)], wor_s, wor_r).wait_send()
    whole(wo.at[pl.ds(0, 4)], woc_s, woc_r).wait_send()
    for k, w in enumerate((wg, wu, wd)):
        whole(w.at[pl.ds(0, 3)], wf_s.at[k], wf_r.at[k]).wait_send()
        whole(w.at[pl.ds(0, 4)], wfc_s.at[k], wfc_r.at[k]).wait_send()
    whole(precv.at[pl.ds(0, REQS - 1)], rs1_s, rs1_r).wait_send()
    whole(qall.at[pl.ds(0, NS - 1)], ag1_s, ag1_r).wait_send()
    whole(arecv.at[pl.ds(0, NS - 1)], rs2_s, rs2_r).wait_send()
    whole(orecv.at[pl.ds(0, NZ - 1)], rs3_s, rs3_r).wait_send()
    whole(xall.at[pl.ds(0, NS - 1)], ag2_s, ag2_r).wait_send()
    whole(drecv.at[pl.ds(0, NS - 1)], rs4_s, rs4_r).wait_send()

    whole(lall.at[pl.ds(0, NS - 1)], ag3_s, ag3_r).wait_recv()
    xf[...] = lall[...].astype(F32)
    for j in range(DR):
        out_ref[:, LANES * j : LANES * (j + 1)] = xf[:, j, :].astype(BF16)
    whole(lall.at[pl.ds(0, NS - 1)], ag3_s, ag3_r).wait_send()


def on_device(
    hidden_in, attn_gain, q_gain, k_gain, post_attn_gain, ffn_gain, post_ffn_gain,
    w_qkv, w_out, w_gate, w_up, w_down,
    prompt_keys, prompt_values, tail_keys, tail_values,
    group_of, prompt_lengths, tail_lengths, page_table,
):
    vmem = pl.BlockSpec(memory_space=pltpu.VMEM)
    hbm = pl.BlockSpec(memory_space=pltpu.HBM)
    dma = pltpu.SemaphoreType.DMA
    scratch = [
        pltpu.VMEM((REQS, STEPS, D), BF16),
        pltpu.VMEM((1, D), F32),
        pltpu.VMEM((2, LANES), F32),
        pltpu.VMEM((2, LANES), F32),
        pltpu.VMEM((DR, LANES), F32),
        pltpu.VMEM((DR, LANES), F32),
        pltpu.VMEM((DR, LANES), F32),
        pltpu.VMEM((1, REQS), jnp.int32),
        pltpu.VMEM((1, 2), jnp.int32),
        pltpu.VMEM((1, REQS), jnp.int32),
        pltpu.VMEM((1, 1024), jnp.int32),
        pltpu.VMEM((T, D), F32),
        pltpu.VMEM((T, DR, LANES), F32),
        pltpu.VMEM((T, D), BF16),
        pltpu.VMEM((512, 512), BF16),
        pltpu.VMEM((512, 512), BF16),
        pltpu.VMEM((T, 512), F32),
        pltpu.VMEM((32, 384), BF16),
        pltpu.VMEM((256, 384), BF16),
        pltpu.VMEM((NR, 256, 256), BF16),
        pltpu.VMEM((NR, 256, LANES), BF16),
        pltpu.VMEM((NR, 256, LANES), BF16),
        pltpu.VMEM((NR, LANES, 256), BF16),
        pltpu.VMEM((REQS, STEPS, 384), F32),
        pltpu.VMEM((REQS, STEPS, 384), F32),
        pltpu.VMEM((NS, STEPS, 768), BF16),
        pltpu.VMEM((12 * T, HD), F32),
        pltpu.VMEM((NS, 8, HD + LANES), BF16),
        pltpu.VMEM((NS, 8, HD + LANES), BF16),
        pltpu.VMEM((NZ, DR, LANES), F32),
        pltpu.VMEM((NZ, DR, LANES), F32),
        pltpu.VMEM((DR, LANES), BF16),
        pltpu.VMEM((T, DR, LANES), BF16),
        pltpu.VMEM((T, DR, LANES), F32),
        pltpu.VMEM((T, D), BF16),
        pltpu.VMEM((T, DR, LANES), F32),
        pltpu.VMEM((T, DR, LANES), BF16),
        pltpu.VMEM((NS, DR, LANES), BF16),
        pltpu.VMEM((DR, LANES), BF16),
        pltpu.VMEM((T, DR, LANES), BF16),
        dma((22,)),
        dma, dma, dma, dma, dma, dma, dma, dma, dma((3,)), dma((3,)), dma((3,)), dma((3,)),
        dma, dma, dma, dma, dma, dma, dma, dma,
        dma, dma, dma, dma, dma, dma,
    ]
    out = pl.pallas_call(
        kernel,
        name="decode_layer",
        out_shape=jax.ShapeDtypeStruct((T, D), BF16),
        in_specs=[hbm] * 20,
        out_specs=vmem,
        scratch_shapes=scratch,
        compiler_params=pltpu.CompilerParams(
            collective_id=0, has_side_effects=True, vmem_limit_bytes=40 << 20
        ),
    )(*[pltpu.with_memory_space_constraint(a, pltpu.HBM) for a in (
        hidden_in,
        attn_gain.reshape(1, D),
        q_gain.reshape(2, LANES),
        k_gain.reshape(2, LANES),
        post_attn_gain.reshape(DR, LANES),
        ffn_gain.reshape(DR, LANES),
        post_ffn_gain.reshape(DR, LANES),
        w_qkv, w_out, w_gate, w_up, w_down,
        prompt_keys, prompt_values, tail_keys, tail_values,
        group_of.reshape(1, REQS),
        prompt_lengths.reshape(1, 2),
        tail_lengths.reshape(1, REQS),
        page_table,
    )])
    return out.reshape(REQS, STEPS, D)


def solution(mesh):
    return jax.shard_map(
        on_device,
        mesh=mesh,
        in_specs=(
            P("req", None, None),
            P(), P(), P(), P(), P(), P(),
            P("seq", "req"),
            P("seq", "req"),
            P("req", "seq"),
            P("req", "seq"),
            P("seq", "req"),
            P("req", "seq", None),
            P("req", "seq", None),
            P("req", "seq", None),
            P("req", "seq", None),
            P("req"), P("req"), P("req"),
            P("req", None),
        ),
        out_specs=P("req", None, None),
        check_vma=False,
    )
```

```python
import jax
import jax.numpy as jnp
from jax import lax
from jax.experimental import pallas as pl
from jax.experimental.pallas import tpu as pltpu
from jax.sharding import PartitionSpec as P

MESH = pl.DeviceIdType.MESH
D = 2048
H = 8
KV = 2
HD = 256
PAGE = 16
QKV = 3072
NZ = 8
NY = 8
NS = 64
NR = 8
T = 64
STEPS = 4
REQS = 16
LANES = 128
DR = D // LANES
QR = QKV // LANES
EPSILON = 1e-06
NEGATIVE = -1e30
F32 = jnp.float32
BF16 = jnp.bfloat16
NT = (((1,), (1,)), ((), ()))


def iota(shape, dim):
    return lax.broadcasted_iota(jnp.int32, shape, dim)


def row_norm(row):
    total = jnp.sum(jnp.sum(row * row, axis=1, keepdims=True), axis=0, keepdims=True)
    return row * lax.rsqrt(total / D + EPSILON)


def kernel(
    hid_hbm, again_hbm, qgain_hbm, kgain_hbm, pagain_hbm, fgain_hbm, pfgain_hbm,
    wqkv_ref, wout_ref, wgate_ref, wup_ref, wdown_ref,
    pk_ref, pv_ref, tk_ref, tv_ref,
    grp_hbm, plen_hbm, tlen_hbm, table_hbm,
    out_ref,
    hid_ref, again_ref, qgain_ref, kgain_ref, pagain_ref, fgain_ref, pfgain_ref,
    grp_ref, plen_ref, tlen_ref, table_ref,
    hf, hid3, nb, kbuf, vbuf, maskf,
    wown, wq, wo, wg, wu, wd,
    psend, precv, qall, q2f,
    asend, arecv, of, orecv, xrow, xall, xf, x2,
    df, dsend, drecv, lrow, lall,
    local_sem, wq_s, wq_r, woy_s, woy_r, wor_s, wor_r, woc_s, woc_r, wf_s, wf_r, wfc_s, wfc_r,
    rs1_s, rs1_r, ag1_s, ag1_r, rs2_s, rs2_r, rs3_s, rs3_r,
    ag2_s, ag2_r, rs4_s, rs4_r, ag3_s, ag3_r,
):
    s = lax.axis_index("seq")
    r = lax.axis_index("req")
    z = s // NY
    y = s % NY
    token = y * NZ + z
    chunk = (y + r) % NY
    core = r % 2
    slot = core * 4 + r // 2
    sibling = (s, r + 1 - 2 * core)

    def seq_dev(zz, yy):
        return (zz * NY + yy, r)

    def req_dev(i):
        return (s, (r + i) % NR)

    rows_y = [(y + k) % NY for k in (4, 3, 5, 2, 0, 6, 1, 7)]

    def each_seq(fn):
        def line(i, carry):
            zz = (z + NZ // 2 + i) % NZ
            for yy in rows_y:
                fn(zz, yy)
            return carry

        lax.fori_loop(0, NZ // 2 - 1, line, 0)
        lax.fori_loop(NZ // 2 + 1, NZ, line, 0)
        line(NZ // 2 - 1, 0)
        for k, yy in enumerate(rows_y):
            if k != NY // 2:
                fn(z, yy)

    def copy(src, dst, ssem, rsem, dev):
        return pltpu.make_async_remote_copy(
            src_ref=src, dst_ref=dst, send_sem=ssem, recv_sem=rsem,
            device_id=dev, device_id_type=MESH,
        )

    def whole(ref, ssem, rsem):
        return copy(ref, ref, ssem, rsem, req_dev(1))

    pairs = [
        (hid_hbm, hid_ref),
        (again_hbm, again_ref),
        (wqkv_ref, wown),
        (wout_ref, wo.at[slot, pl.ds(y * 32, 32)]),
        (wgate_ref, wg.at[slot]),
        (wup_ref, wu.at[slot]),
        (wdown_ref, wd.at[slot]),
        (grp_hbm, grp_ref),
        (plen_hbm, plen_ref),
        (tlen_hbm, tlen_ref),
        (table_hbm, table_ref),
        (qgain_hbm, qgain_ref),
        (kgain_hbm, kgain_ref),
        (pagain_hbm, pagain_ref),
        (fgain_hbm, fgain_ref),
        (pfgain_hbm, pfgain_ref),
        (pk_ref.at[0], kbuf.at[pl.ds(0, 128)]),
        (pk_ref.at[1], kbuf.at[pl.ds(128, 128)]),
        (tk_ref.at[0], kbuf.at[pl.ds(256, 256)]),
        (pv_ref.at[0], vbuf.at[pl.ds(0, 128)]),
        (pv_ref.at[1], vbuf.at[pl.ds(128, 128)]),
        (tv_ref.at[0], vbuf.at[pl.ds(256, 256)]),
    ]
    loads = [pltpu.make_async_copy(a, b, local_sem.at[i]) for i, (a, b) in enumerate(pairs)]
    for ld in loads:
        ld.start()

    barrier = pltpu.get_barrier_semaphore()

    def meet(dev):
        pl.semaphore_signal(barrier, inc=1, device_id=dev, device_id_type=MESH)

    partner = (chunk + 1 - 2 * (chunk % 2) + NR - r) % NY
    for i in range(1, NY):
        meet(seq_dev(z, (y + i) % NY))
        meet(seq_dev((z + i) % NZ, y))
    for i in range(NZ):
        meet(seq_dev((z + i) % NZ, partner))
    for i in range(1, 4):
        meet((s, (r + 2 * i) % NR))
    meet(sibling)

    for i in range(1, NR):
        meet((z * NY + NY - i, (r + i) % NR))
        meet((z * NY + (y + i) % NY, chunk))
    pl.when(y != 0)(lambda: meet((z * NY, r)))
    pl.when(y != 0)(lambda: meet((s, chunk)))

    for ld in loads[:2]:
        ld.wait()
    for i in range(REQS):
        hf[STEPS * i : STEPS * (i + 1), :] = hid_ref[i].astype(F32)
    hidden = hf[...]
    scale = lax.rsqrt(jnp.mean(hidden * hidden, axis=1, keepdims=True) + EPSILON)
    nb[...] = (hidden * scale * again_ref[...]).astype(BF16)
    for j in range(DR):
        hid3[:, j, :] = hf[:, LANES * j : LANES * (j + 1)]

    peers = 2 * (NY - 1) + NZ + 4 + 2 * (NR - 1)
    pl.when(y == 0)(lambda: pl.semaphore_wait(barrier, peers))
    pl.when(y != 0)(lambda: pl.semaphore_wait(barrier, peers + 2))

    loads[2].wait()
    rows_here = wq.at[pl.ds(y * 32, 32)]
    for i in range(1, NR):
        copy(wown, rows_here, wq_s, wq_r, (z * NY + NY - i, (r + i) % NR)).start()

    @pl.when(y != 0)
    def _():
        copy(wown, rows_here, wq_s, wq_r, (z * NY, r)).start()

    @pl.when(y == 0)
    def _():
        wq[pl.ds(pl.multiple_of(y * 32, 32), 32), :] = wown[...]

    x256 = nb[:, pl.ds(pl.multiple_of(z * 256, 256), 256)]

    @pl.when(y != 0)
    def _():
        whole(wq, wq_s, wq_r).wait_recv()

    @pl.when(y == 0)
    def _():
        whole(wq.at[pl.ds(0, 224)], wq_s, wq_r).wait_recv()

    part = jnp.dot(x256, wq[...], preferred_element_type=F32)
    for i in range(REQS):
        psend[i] = part[STEPS * i : STEPS * (i + 1), :]
    odd = chunk % 2
    quad = chunk // 2
    own_request = 2 * z + odd
    source = odd * NZ + z
    precv[source] = psend[own_request]
    for i in range(NZ):
        zz = (z + NZ // 2 + i) % NZ
        for b in range(2):
            if i == NZ // 2 and b == 0:
                continue
            other = (odd + b) % 2
            copy(
                psend.at[2 * zz + other], precv.at[source], rs1_s, rs1_r,
                seq_dev(zz, (2 * quad + other + NR - r) % NY),
            ).start()

    def over_x(w, ssem, rsem):
        for i in range(1, 4):
            copy(w.at[slot], w.at[slot], ssem, rsem, (s, (r + 2 * i) % NR)).start()

    def over_core(w, ssem, rsem):
        half = w.at[pl.ds(core * 4, 4)]
        copy(half, half, ssem, rsem, sibling).start()

    for ld in loads[3:7]:
        ld.wait()
    mine = wo.at[slot, pl.ds(y * 32, 32)]
    for i in range(1, NY):
        copy(mine, mine, woy_s, woy_r, seq_dev(z, (y + i) % NY)).start()
    over_x(wg, wf_s.at[0], wf_r.at[0])

    for ld in loads[7:16]:
        ld.wait()
    req_of = iota((T, REQS), 0) // STEPS == iota((T, REQS), 1)
    group = jnp.sum(
        jnp.where(req_of, (grp_ref[...] % 2).astype(F32), 0.0), axis=1, keepdims=True
    )
    tail_len = jnp.sum(jnp.where(req_of, tlen_ref[...].astype(F32), 0.0), axis=1, keepdims=True)
    lanes = iota((T, 256), 1)
    plen = jnp.where(lanes < 128, plen_ref[:, 0:1], plen_ref[:, 1:2])
    prompt_live = (s * 128 + lanes % 128 < plen) & (group == (lanes // 128).astype(F32))
    match = (table_ref[...] == s * 16 + iota((256, 1024), 0) // PAGE).astype(F32).astype(BF16)
    entry = iota((8, 1024), 1)
    digits = jnp.where(iota((8, 1024), 0) == 0, entry // 64, entry % 64)
    found = lax.dot_general(
        digits.astype(F32).astype(BF16), match, NT, preferred_element_type=F32
    )
    owner = found[0:1, :]
    position = found[1:2, :] * PAGE + (iota((1, 256), 1) % PAGE).astype(F32)
    own_req = (iota((T, 256), 0) // STEPS).astype(F32)
    tail_live = (owner == own_req) & (position < tail_len)
    maskf[:, 0:256] = jnp.where(prompt_live, 1.0, 0.0)
    maskf[:, 256:512] = jnp.where(tail_live, 1.0, 0.0)

    whole(precv.at[pl.ds(0, REQS - 1)], rs1_s, rs1_r).wait_recv()
    low = jnp.sum(precv[0:NZ], axis=0)
    high = jnp.sum(precv[NZ : 2 * NZ], axis=0)
    chunks = [low[:, LANES * u : LANES * (u + 1)] for u in range(3)]
    chunks += [high[:, LANES * u : LANES * (u + 1)] for u in range(3)]
    pieces = []
    for i in range(3):
        pair = chunks[2 * i : 2 * i + 2]
        mean = sum(jnp.sum(c * c, axis=1, keepdims=True) for c in pair) / HD
        inverse = lax.rsqrt(mean + EPSILON)
        head = 3 * quad + i
        for u in range(2):
            gain = jnp.where(
                head < H,
                qgain_ref[u : u + 1, :],
                jnp.where(head < H + KV, kgain_ref[u : u + 1, :], 1.0),
            )
            pieces.append(pair[u] * inverse * gain)
    place = own_request * 4 + quad
    qall[place] = jnp.concatenate(pieces, axis=1).astype(BF16)

    def send_ag1(zz, yy):
        copy(qall.at[place], qall.at[place], ag1_s, ag1_r, seq_dev(zz, yy)).start()

    each_seq(send_ag1)
    whole(wo.at[0, pl.ds(0, 224)], woy_s, woy_r).wait_recv()
    over_x(wo, wor_s, wor_r)
    over_x(wu, wf_s.at[1], wf_r.at[1])
    over_x(wd, wf_s.at[2], wf_r.at[2])
    for ld in loads[16:]:
        ld.wait()
    whole(qall.at[pl.ds(0, NS - 1)], ag1_s, ag1_r).wait_recv()
    for i in range(REQS):
        for k in range(4):
            block = qall[4 * i + k].astype(F32)
            for u in range(3):
                top = T * (3 * k + u) + STEPS * i
                q2f[top : top + STEPS, :] = block[:, HD * u : HD * (u + 1)]

    mask = maskf[...]
    mask4 = jnp.concatenate([mask, mask, mask, mask], axis=0) > 0.5
    rows = H // KV * T
    for c in range(KV):
        heads = q2f[rows * c : rows * (c + 1), :].astype(BF16)
        scores = lax.dot_general(
            heads, kbuf[:, HD * c : HD * (c + 1)], NT, preferred_element_type=F32
        )
        scores = jnp.where(mask4, scores, NEGATIVE)
        top = jnp.max(scores, axis=1, keepdims=True)
        probs = jnp.where(mask4, jnp.exp(scores - top), 0.0)
        total = jnp.sum(probs, axis=1, keepdims=True)
        accum = jnp.dot(
            probs.astype(BF16), vbuf[:, HD * c : HD * (c + 1)], preferred_element_type=F32
        )
        lane = iota((rows, LANES), 1)
        stats = jnp.zeros((rows, LANES), F32)
        for base, rest in ((0, top), (3, total)):
            for k in range(3):
                high = rest.astype(BF16).astype(F32)
                stats = jnp.where(lane == base + k, high, stats)
                rest = rest - high
        eight = rows // 8
        asend[eight * c : eight * (c + 1), :, 0:HD] = accum.reshape(eight, 8, HD).astype(BF16)
        asend[eight * c : eight * (c + 1), :, HD : HD + LANES] = stats.reshape(
            eight, 8, LANES
        ).astype(BF16)

    arecv[s] = asend[s]

    def send_rs2(zz, yy):
        copy(asend.at[zz * NY + yy], arecv.at[s], rs2_s, rs2_r, seq_dev(zz, yy)).start()

    each_seq(send_rs2)
    whole(wo.at[pl.ds(0, 3)], wor_s, wor_r).wait_recv()
    over_core(wo, woc_s, woc_r)
    for k, w in enumerate((wg, wu, wd)):
        whole(w.at[pl.ds(0, 3)], wf_s.at[k], wf_r.at[k]).wait_recv()
        over_core(w, wfc_s.at[k], wfc_r.at[k])

    def eight_of(head):
        return q2f[pl.ds(pl.multiple_of(head * T + y * 8, 8), 8), :]

    q8 = eight_of(z).astype(BF16)
    k8 = eight_of(H + z // 4).astype(BF16)
    v8 = eight_of(H + KV + z // 4)
    new_scores = lax.dot_general(q8, k8, NT, preferred_element_type=F32)
    qi = iota((8, 8), 0)
    ki = iota((8, 8), 1)
    causal = (qi // STEPS == ki // STEPS) & (ki <= qi)
    new_scores = jnp.where(causal, new_scores, NEGATIVE)
    new_top = jnp.max(new_scores, axis=1, keepdims=True)

    whole(arecv.at[pl.ds(0, NS - 1)], rs2_s, rs2_r).wait_recv()
    stats = arecv[:, :, HD : HD + LANES].astype(F32)
    tops = stats[:, :, 0:1] + stats[:, :, 1:2] + stats[:, :, 2:3]
    totals = stats[:, :, 3:4] + stats[:, :, 4:5] + stats[:, :, 5:6]
    highest = jnp.maximum(jnp.max(tops, axis=0), new_top)
    weight = jnp.exp(tops - highest[None])
    new_probs = jnp.where(causal, jnp.exp(new_scores - highest), 0.0)
    denominator = jnp.sum(totals * weight, axis=0) + jnp.sum(new_probs, axis=1, keepdims=True)
    numerator = jnp.sum(arecv[:, :, 0:HD].astype(F32) * weight, axis=0) + jnp.dot(
        new_probs, v8, preferred_element_type=F32, precision=lax.Precision.HIGHEST
    )
    attention = (numerator / denominator).astype(BF16)

    whole(wo.at[pl.ds(0, 4)], woc_s, woc_r).wait_recv()
    for k in range(NR):
        part = jnp.dot(attention, wo[k % 2 * 4 + k // 2], preferred_element_type=F32)
        for u in range(2):
            of[:, 2 * k + u, :] = part[:, LANES * u : LANES * (u + 1)]
    orecv[z] = of[z]
    for i in range(1, NZ):
        zz = (z + i) % NZ
        copy(of.at[zz], orecv.at[z], rs3_s, rs3_r, seq_dev(zz, y)).start()
    whole(orecv.at[pl.ds(0, NZ - 1)], rs3_s, rs3_r).wait_recv()
    out_row = jnp.sum(orecv[...], axis=0)
    residual = hid3[token] + row_norm(out_row) * pagain_ref[...]
    xrow[...] = (row_norm(residual) * fgain_ref[...]).astype(BF16)
    xall[token] = xrow[...]

    def send_ag2(zz, yy):
        copy(xrow, xall.at[token], ag2_s, ag2_r, seq_dev(zz, yy)).start()

    each_seq(send_ag2)
    for k, w in enumerate((wg, wu, wd)):
        whole(w.at[pl.ds(0, 4)], wfc_s.at[k], wfc_r.at[k]).wait_recv()
    whole(xall.at[pl.ds(0, NS - 1)], ag2_s, ag2_r).wait_recv()

    xf[...] = xall[...].astype(F32)
    for j in range(DR):
        x2[:, LANES * j : LANES * (j + 1)] = xf[:, j, :].astype(BF16)
    gate = jnp.zeros((T, LANES), F32)
    up = jnp.zeros((T, LANES), F32)
    for k in range(NR):
        xk = x2[:, 256 * k : 256 * (k + 1)]
        gate = gate + jnp.dot(xk, wg[k % 2 * 4 + k // 2], preferred_element_type=F32)
        up = up + jnp.dot(xk, wu[k % 2 * 4 + k // 2], preferred_element_type=F32)
    activated = (jax.nn.gelu(gate, approximate=True) * up).astype(BF16)
    for k in range(NR):
        part = jnp.dot(activated, wd[k % 2 * 4 + k // 2], preferred_element_type=F32)
        for u in range(2):
            df[:, 2 * k + u, :] = part[:, LANES * u : LANES * (u + 1)]
    dsend[...] = df[...].astype(BF16)
    drecv[s] = dsend[token]

    def send_rs4(zz, yy):
        copy(dsend.at[yy * NZ + zz], drecv.at[s], rs4_s, rs4_r, seq_dev(zz, yy)).start()

    each_seq(send_rs4)
    whole(drecv.at[pl.ds(0, NS - 1)], rs4_s, rs4_r).wait_recv()
    down = jnp.sum(drecv[...].astype(F32), axis=0)
    lrow[...] = (residual + row_norm(down) * pfgain_ref[...]).astype(BF16)
    lall[token] = lrow[...]

    def send_ag3(zz, yy):
        copy(lrow, lall.at[token], ag3_s, ag3_r, seq_dev(zz, yy)).start()

    each_seq(send_ag3)

    whole(wq.at[pl.ds(0, 224)], wq_s, wq_r).wait_send()
    pl.when(y != 0)(lambda: whole(wq.at[pl.ds(0, 32)], wq_s, wq_r).wait_send())
    whole(wo.at[0, pl.ds(0, 224)], woy_s, woy_r).wait_send()
    whole(wo.at[pl.ds(0, 3)], wor_s, wor_r).wait_send()
    whole(wo.at[pl.ds(0, 4)], woc_s, woc_r).wait_send()
    for k, w in enumerate((wg, wu, wd)):
        whole(w.at[pl.ds(0, 3)], wf_s.at[k], wf_r.at[k]).wait_send()
        whole(w.at[pl.ds(0, 4)], wfc_s.at[k], wfc_r.at[k]).wait_send()
    whole(precv.at[pl.ds(0, REQS - 1)], rs1_s, rs1_r).wait_send()
    whole(qall.at[pl.ds(0, NS - 1)], ag1_s, ag1_r).wait_send()
    whole(arecv.at[pl.ds(0, NS - 1)], rs2_s, rs2_r).wait_send()
    whole(orecv.at[pl.ds(0, NZ - 1)], rs3_s, rs3_r).wait_send()
    whole(xall.at[pl.ds(0, NS - 1)], ag2_s, ag2_r).wait_send()
    whole(drecv.at[pl.ds(0, NS - 1)], rs4_s, rs4_r).wait_send()

    whole(lall.at[pl.ds(0, NS - 1)], ag3_s, ag3_r).wait_recv()
    xf[...] = lall[...].astype(F32)
    for j in range(DR):
        out_ref[:, LANES * j : LANES * (j + 1)] = xf[:, j, :].astype(BF16)
    whole(lall.at[pl.ds(0, NS - 1)], ag3_s, ag3_r).wait_send()


def on_device(
    hidden_in, attn_gain, q_gain, k_gain, post_attn_gain, ffn_gain, post_ffn_gain,
    w_qkv, w_out, w_gate, w_up, w_down,
    prompt_keys, prompt_values, tail_keys, tail_values,
    group_of, prompt_lengths, tail_lengths, page_table,
):
    vmem = pl.BlockSpec(memory_space=pltpu.VMEM)
    hbm = pl.BlockSpec(memory_space=pltpu.HBM)
    dma = pltpu.SemaphoreType.DMA
    scratch = [
        pltpu.VMEM((REQS, STEPS, D), BF16),
        pltpu.VMEM((1, D), F32),
        pltpu.VMEM((2, LANES), F32),
        pltpu.VMEM((2, LANES), F32),
        pltpu.VMEM((DR, LANES), F32),
        pltpu.VMEM((DR, LANES), F32),
        pltpu.VMEM((DR, LANES), F32),
        pltpu.VMEM((1, REQS), jnp.int32),
        pltpu.VMEM((1, 2), jnp.int32),
        pltpu.VMEM((1, REQS), jnp.int32),
        pltpu.VMEM((1, 1024), jnp.int32),
        pltpu.VMEM((T, D), F32),
        pltpu.VMEM((T, DR, LANES), F32),
        pltpu.VMEM((T, D), BF16),
        pltpu.VMEM((512, 512), BF16),
        pltpu.VMEM((512, 512), BF16),
        pltpu.VMEM((T, 512), F32),
        pltpu.VMEM((32, 384), BF16),
        pltpu.VMEM((256, 384), BF16),
        pltpu.VMEM((NR, 256, 256), BF16),
        pltpu.VMEM((NR, 256, LANES), BF16),
        pltpu.VMEM((NR, 256, LANES), BF16),
        pltpu.VMEM((NR, LANES, 256), BF16),
        pltpu.VMEM((REQS, STEPS, 384), F32),
        pltpu.VMEM((REQS, STEPS, 384), F32),
        pltpu.VMEM((NS, STEPS, 768), BF16),
        pltpu.VMEM((12 * T, HD), F32),
        pltpu.VMEM((NS, 8, HD + LANES), BF16),
        pltpu.VMEM((NS, 8, HD + LANES), BF16),
        pltpu.VMEM((NZ, DR, LANES), F32),
        pltpu.VMEM((NZ, DR, LANES), F32),
        pltpu.VMEM((DR, LANES), BF16),
        pltpu.VMEM((T, DR, LANES), BF16),
        pltpu.VMEM((T, DR, LANES), F32),
        pltpu.VMEM((T, D), BF16),
        pltpu.VMEM((T, DR, LANES), F32),
        pltpu.VMEM((T, DR, LANES), BF16),
        pltpu.VMEM((NS, DR, LANES), BF16),
        pltpu.VMEM((DR, LANES), BF16),
        pltpu.VMEM((T, DR, LANES), BF16),
        dma((22,)),
        dma, dma, dma, dma, dma, dma, dma, dma, dma((3,)), dma((3,)), dma((3,)), dma((3,)),
        dma, dma, dma, dma, dma, dma, dma, dma,
        dma, dma, dma, dma, dma, dma,
    ]
    out = pl.pallas_call(
        kernel,
        name="decode_layer",
        out_shape=jax.ShapeDtypeStruct((T, D), BF16),
        in_specs=[hbm] * 20,
        out_specs=vmem,
        scratch_shapes=scratch,
        compiler_params=pltpu.CompilerParams(
            collective_id=0, has_side_effects=True, vmem_limit_bytes=40 << 20
        ),
    )(*[pltpu.with_memory_space_constraint(a, pltpu.HBM) for a in (
        hidden_in,
        attn_gain.reshape(1, D),
        q_gain.reshape(2, LANES),
        k_gain.reshape(2, LANES),
        post_attn_gain.reshape(DR, LANES),
        ffn_gain.reshape(DR, LANES),
        post_ffn_gain.reshape(DR, LANES),
        w_qkv, w_out, w_gate, w_up, w_down,
        prompt_keys, prompt_values, tail_keys, tail_values,
        group_of.reshape(1, REQS),
        prompt_lengths.reshape(1, 2),
        tail_lengths.reshape(1, REQS),
        page_table,
    )])
    return out.reshape(REQS, STEPS, D)


def solution(mesh):
    return jax.shard_map(
        on_device,
        mesh=mesh,
        in_specs=(
            P("req", None, None),
            P(), P(), P(), P(), P(), P(),
            P("seq", "req"),
            P("seq", "req"),
            P("req", "seq"),
            P("req", "seq"),
            P("seq", "req"),
            P("req", "seq", None),
            P("req", "seq", None),
            P("req", "seq", None),
            P("req", "seq", None),
            P("req"), P("req"), P("req"),
            P("req", None),
        ),
        out_specs=P("req", None, None),
        check_vma=False,
    )
```
